512 devices in a mesh: row: 16 (over y, x), col: 32 (over z, core).
Axes of the slice: x: 4, y: 4, z: 16, core: 2. Of those that a mesh axis runs over, the one named last changes fastest.
Arguments:
- root_inverse: bfloat16 [4096, 4096], P('row', 'col'), may hold values from -16 to 16
- factor: bfloat16 [4096, 4, 4096], P('row', None, 'col'), may hold values from -0.59765625 to 0.59765625
- inverse_diag: bfloat16 [4096, 4, 4096], P('row', None, 'col'), may hold values from -6 to 6
- structure: int32 [4, 32], replicated, may hold values 0 or 1
Outputs:
- ainv_rk: bfloat16 [4096, 4, 4096], P('row', None, 'col')
- ainv_kk: bfloat16 [4096, 4, 4096], P('row', None, 'col')
The draws below stay inside these ranges and needn't reach their ends.
All inputs are finite; a program needn't handle non-finite values.
Results may differ from the reference program's by a relative error of at most 0.014.
Values may be sent and summed in bfloat16 or wider, within the bound.
No kernel may reach another device: no remote copies, remote signals or barrier semaphores. Data moves between devices by JAX's collectives and lax.ppermute only.
A program may use at most 64 MiB of HBM per device.

```python
import math
import jax
import jax.numpy as jnp
from jax import lax

W = 4096
BLK = 128
NKID = 4
NBLK = 32
N_ROW = 16


def draw_root_inverse(key, part):
    noise_draw = jax.random.normal(key, (W, W), jnp.float32)
    symmetric = (noise_draw + noise_draw.T) * (0.7071 / math.sqrt(W))
    matrix = symmetric + 1.5 * jnp.eye(W, dtype=jnp.float32)
    return matrix.astype(jnp.bfloat16)


def place_ends(result, key, least, top_value):
    dims = result.shape
    place = [jax.random.randint(jax.random.fold_in(key, axis), (), 0, dims[axis]) for axis in range(len(dims))]
    result = result.at[tuple(place)].set(least)
    longest = dims.index(max(dims))
    place[longest] = (place[longest] + 1) % dims[longest]
    return result.at[tuple(place)].set(top_value)


def block_levels(rng, dims, split, least, largest):
    level = 1.0
    for axis_at, blocks in split:
        draws = jax.random.uniform(jax.random.fold_in(jax.random.fold_in(rng, 6), axis_at), (blocks,), jnp.float32, least / len(split), largest / len(split))
        level = level * jnp.repeat(jnp.exp(draws), dims[axis_at] // blocks).reshape((-1,) + (1,) * (len(dims) - 1 - axis_at))
    return level


def noise(key, dims, deviation, bound, shards=(), held_as=jnp.bfloat16):
    level = block_levels(key, dims, shards, -0.22, 0.18) if shards else 1.0
    entries = jax.random.normal(key, dims, jnp.float32) * deviation * level
    return jnp.minimum(jnp.maximum(entries, -bound), bound).astype(held_as)


def setup_inputs(seed: int = 0) -> dict:
    key_of = jax.random.split(jax.random.key(seed), 5)
    return {
        "root_inverse": draw_root_inverse(jax.random.fold_in(key_of[4], 71), 0),
        "factor": noise(key_of[1], (W, NKID, W), 0.1, 0.59765625, ((0, 16), (2, 32))),
        "inverse_diag": noise(key_of[2], (W, NKID, W), 1.0, 6.0, ((0, 16), (2, 32))),
        "structure": place_ends((jax.random.randint(key_of[3], (NKID, NBLK), 0, 4) < 3).astype(jnp.int32), jax.random.fold_in(key_of[3], 1), 0, 1),
    }


def reference(root_inverse, factor, inverse_diag, structure):
    row_mask = jnp.repeat(structure, BLK, axis=1).T.astype(factor.dtype)
    masked = factor * row_mask[:, :, None]
    product = jnp.einsum('ik,knj->inj', root_inverse.astype(jnp.float32), masked.astype(jnp.float32), precision=lax.Precision.HIGHEST)
    ainv_rk = (-product).astype(jnp.bfloat16)
    group_rows = W // N_ROW
    masked_wide = masked.astype(jnp.float32)
    inverse_wide = ainv_rk.astype(jnp.float32)

    def add_group(group, running):
        offset = (group * group_rows).astype(jnp.int32)
        left_part = lax.dynamic_slice_in_dim(masked_wide, offset, group_rows, 0)
        right_part = lax.dynamic_slice_in_dim(inverse_wide, offset, group_rows, 0)
        term = jnp.einsum('kni,knj->inj', left_part, right_part, precision=lax.Precision.HIGHEST)
        return running + term.astype(jnp.bfloat16).astype(jnp.float32)

    running = jnp.zeros(inverse_diag.shape, jnp.float32)
    running = lax.fori_loop(0, N_ROW, add_group, running)
    ainv_kk = (inverse_diag.astype(jnp.float32) - running).astype(jnp.bfloat16)
    return ainv_rk, ainv_kk
```

```python
import jax
import jax.numpy as jnp
from jax import lax
from jax.experimental import pallas as pl
from jax.experimental.pallas import tpu as pltpu
from jax.sharding import PartitionSpec as P

BLK = 128
CHUNKS = 8
VMEM_FIRST, VMEM_ROOT, VMEM_KID = 63, 57, 57
ANY = pl.BlockSpec(memory_space=pl.ANY)
VMEM = pl.BlockSpec(memory_space=pltpu.VMEM)
SMEM = pl.BlockSpec(memory_space=pltpu.SMEM)


def split_kids(flat_ref, kids_ref, flat_buf, wide_ref, sem):
    kids, rows, _ = kids_ref.shape
    copy = pltpu.make_async_copy(flat_ref, flat_buf, sem)
    copy.start()
    copy.wait()
    wide_ref[...] = flat_buf[...].astype(jnp.float32)
    for n in range(kids):
        kids_ref[n] = wide_ref[pl.ds(n, rows, stride=kids), :].astype(kids_ref.dtype)


def root_product(
    keep_ref, row_ref, panel_ref, ainv_ref, turned_ref, row_buf, root_buf, acc_ref, wide_ref, sems
):
    n_row, kids, depth, cols = row_buf.shape
    last = panel_ref.shape[1] - 1
    g, c = n_row // CHUNKS, root_buf.shape[0] // CHUNKS

    def row_copy(s):
        return pltpu.make_async_copy(
            row_ref.at[pl.ds(s * g, g)], row_buf.at[pl.ds(s * g, g)], sems.at[0, s]
        )

    def root_copy(s):
        return pltpu.make_async_copy(
            panel_ref.at[pl.ds(s * c, c), last], root_buf.at[pl.ds(s * c, c)], sems.at[1, s]
        )

    for s in range(CHUNKS):
        row_copy(s).start()
        root_copy(s).start()
    acc_ref[...] = jnp.zeros_like(acc_ref)

    @pl.loop(0, CHUNKS)
    def _(s):
        row_copy(s).wait()
        root_copy(s).wait()
        left = jnp.concatenate([root_buf[s * c + i] for i in range(c)], axis=1)
        right = jnp.concatenate(
            [
                jnp.concatenate([row_buf[s * g + i, n] for n in range(kids)], axis=1)
                for i in range(g)
            ],
            axis=0,
        )
        acc_ref[...] += jnp.dot(left, right, preferred_element_type=jnp.float32)

    for n in range(kids):
        value = (-acc_ref[:, n * cols : (n + 1) * cols]).astype(turned_ref.dtype)
        wide_ref[pl.ds(n, depth, stride=kids), :] = value.astype(jnp.float32)
        for b in range(depth // BLK):
            kept = jnp.where(keep_ref[n, b] != 0, value[b * BLK : (b + 1) * BLK], 0)
            turned_ref[n, :, b * BLK : (b + 1) * BLK] = kept.astype(turned_ref.dtype).T
    ainv_ref[...] = wide_ref[...].astype(ainv_ref.dtype)


def kid_product(turned_ref, panel_ref, part_ref, panel_buf, sems):
    n_col, groups, _, _ = panel_buf.shape
    c = n_col // CHUNKS

    def panel_copy(s):
        return pltpu.make_async_copy(
            panel_ref.at[pl.ds(s * c, c), pl.ds(0, groups)],
            panel_buf.at[pl.ds(s * c, c)],
            sems.at[s],
        )

    for s in range(CHUNKS):
        panel_copy(s).start()
    left = jnp.concatenate([turned_ref[y] for y in range(groups)], axis=1)

    @pl.loop(0, CHUNKS)
    def _(s):
        panel_copy(s).wait()
        for i in range(c // 2):
            at = s * c + 2 * i
            right = jnp.concatenate(
                [
                    jnp.concatenate([panel_buf[at + h, y] for y in range(groups)], axis=0)
                    for h in range(2)
                ],
                axis=1,
            )
            part_ref[s * (c // 2) + i] = jnp.dot(
                left, right, preferred_element_type=jnp.float32
            ).astype(part_ref.dtype)


def finish(pieces_ref, diag_ref, kk_ref, wide_ref):
    n_row, _, depth = pieces_ref.shape
    kids = wide_ref.shape[0] // depth
    per = n_row // kids
    wide_ref[...] = diag_ref[...].astype(jnp.float32)
    for n in range(kids):
        total = pieces_ref[n * per].astype(jnp.float32)
        for r in range(1, per):
            total += pieces_ref[n * per + r].astype(jnp.float32)
        at = pl.ds(n, depth, stride=kids)
        wide_ref[at, :] = wide_ref[at, :] - total.T
    kk_ref[...] = wide_ref[...].astype(kk_ref.dtype)


def body(root_inverse, factor, inverse_diag, structure):
    rows, kids, cols = factor.shape
    dtype = factor.dtype
    n_row, n_col = lax.axis_size("row"), lax.axis_size("col")
    per, side = rows // BLK, n_row // kids
    flat = (rows * kids, cols)
    along = [[y * side + x for y in range(kids)] for x in range(side)]
    mine = pl.pallas_call(
        split_kids,
        out_shape=jax.ShapeDtypeStruct((kids, rows, cols), dtype),
        in_specs=[ANY],
        out_specs=VMEM,
        scratch_shapes=[
            pltpu.VMEM(flat, dtype),
            pltpu.VMEM(flat, jnp.float32),
            pltpu.SemaphoreType.DMA(()),
        ],
        compiler_params=pltpu.CompilerParams(vmem_limit_bytes=VMEM_FIRST << 20),
    )(factor.reshape(flat))
    kid = lax.all_to_all(mine, "row", 0, 0, axis_index_groups=along)
    panel = lax.all_gather(jnp.concatenate([kid, root_inverse[None]], axis=0), "col", axis=0)
    keep = lax.dynamic_slice_in_dim(structure, lax.axis_index("row") * per, per, 1)
    mask = jnp.repeat(keep, BLK, axis=1).astype(dtype)
    masked = mine * mask[:, :, None]
    row_m = lax.all_to_all(jnp.broadcast_to(masked[None], (n_row, kids, rows, cols)), "row", 0, 0)
    ainv, turned = pl.pallas_call(
        root_product,
        out_shape=(
            jax.ShapeDtypeStruct(flat, dtype),
            jax.ShapeDtypeStruct((kids, cols, rows), dtype),
        ),
        in_specs=[SMEM, ANY, ANY],
        out_specs=(VMEM, VMEM),
        scratch_shapes=[
            pltpu.VMEM((n_row, kids, rows, cols), dtype),
            pltpu.VMEM((n_col, rows, cols), dtype),
            pltpu.VMEM((rows, kids * cols), jnp.float32),
            pltpu.VMEM(flat, jnp.float32),
            pltpu.SemaphoreType.DMA((2, CHUNKS)),
        ],
        compiler_params=pltpu.CompilerParams(vmem_limit_bytes=VMEM_ROOT << 20),
        cost_estimate=pl.CostEstimate(
            flops=2 * n_row * rows * rows * kids * cols,
            bytes_accessed=6 << 20,
            transcendentals=0,
        ),
    )(keep, row_m, panel)
    turned = lax.all_to_all(turned, "row", 0, 0, axis_index_groups=along)
    part = pl.pallas_call(
        kid_product,
        out_shape=jax.ShapeDtypeStruct((n_row, cols, rows), dtype),
        in_specs=[VMEM, ANY],
        out_specs=VMEM,
        scratch_shapes=[
            pltpu.VMEM((n_col, kids, rows, cols), dtype),
            pltpu.SemaphoreType.DMA((CHUNKS,)),
        ],
        compiler_params=pltpu.CompilerParams(vmem_limit_bytes=VMEM_KID << 20),
        cost_estimate=pl.CostEstimate(
            flops=2 * n_row * rows * rows * kids * cols,
            bytes_accessed=9 << 20,
            transcendentals=0,
        ),
    )(turned, panel)
    pieces = lax.all_to_all(part, "row", 0, 0)
    ainv_kk = pl.pallas_call(
        finish,
        out_shape=jax.ShapeDtypeStruct(flat, dtype),
        in_specs=[VMEM, VMEM],
        out_specs=VMEM,
        scratch_shapes=[pltpu.VMEM(flat, jnp.float32)],
        compiler_params=pltpu.CompilerParams(vmem_limit_bytes=6 << 20),
    )(pieces, inverse_diag.reshape(flat))
    return (ainv.reshape(factor.shape), ainv_kk.reshape(factor.shape))


def solution(mesh):
    return jax.shard_map(
        body,
        mesh=mesh,
        in_specs=(P("row", "col"), P("row", None, "col"), P("row", None, "col"), P()),
        out_specs=(P("row", None, "col"), P("row", None, "col")),
        check_vma=False,
    )
```

```python
import jax
import jax.numpy as jnp
from jax import lax
from jax.experimental import pallas as pl
from jax.experimental.pallas import tpu as pltpu
from jax.sharding import PartitionSpec as P

BLK = 128
CHUNKS = 8
HALVES = 2
VMEM_FIRST, VMEM_ROOT, VMEM_KID = 63, 50, 16
ANY = pl.BlockSpec(memory_space=pl.ANY)
VMEM = pl.BlockSpec(memory_space=pltpu.VMEM)
SMEM = pl.BlockSpec(memory_space=pltpu.SMEM)


def split_kids(flat_ref, root_ref, turned_ref, folded_ref, flat_buf, root_buf, wide_ref, sems):
    groups, half, rows = turned_ref.shape
    kids = groups // HALVES
    cols = root_buf.shape[1]
    flat_copy = pltpu.make_async_copy(flat_ref, flat_buf, sems.at[0])
    root_copy = pltpu.make_async_copy(root_ref, root_buf, sems.at[1])
    flat_copy.start()
    root_copy.start()
    flat_copy.wait()
    wide_ref[...] = flat_buf[...].astype(jnp.float32)
    for n in range(kids):
        across = wide_ref[pl.ds(n, rows, stride=kids), :].astype(turned_ref.dtype).T
        for h in range(HALVES):
            turned_ref[n * HALVES + h] = across[h * half : (h + 1) * half]
    root_copy.wait()
    folded_ref[:, :cols] = root_buf[: rows // 2]
    folded_ref[:, cols:] = root_buf[rows // 2 :]


def root_product(
    keep_ref, row_ref, panel_ref, ainv_ref, slots_ref, row_buf, root_buf, acc_ref, wide_ref, sems
):
    n_row, kids, depth, cols = row_buf.shape
    first = panel_ref.shape[1] - root_buf.shape[1]
    g, c = n_row // CHUNKS, root_buf.shape[0] // CHUNKS

    def row_copy(s):
        return pltpu.make_async_copy(
            row_ref.at[pl.ds(s * g, g)], row_buf.at[pl.ds(s * g, g)], sems.at[0, s]
        )

    def root_copy(s):
        return pltpu.make_async_copy(
            panel_ref.at[pl.ds(s * c, c), pl.ds(first, root_buf.shape[1])],
            root_buf.at[pl.ds(s * c, c)],
            sems.at[1, s],
        )

    for s in range(CHUNKS):
        row_copy(s).start()
        root_copy(s).start()
    acc_ref[...] = jnp.zeros_like(acc_ref)

    @pl.loop(0, CHUNKS)
    def _(s):
        row_copy(s).wait()
        root_copy(s).wait()
        left = jnp.concatenate(
            [
                jnp.concatenate(
                    [root_buf[s * c + i, :, h * cols : (h + 1) * cols] for i in range(c)], axis=1
                )
                for h in range(2)
            ],
            axis=0,
        )
        right = jnp.concatenate(
            [
                jnp.concatenate([row_buf[s * g + i, n] for n in range(kids)], axis=1)
                for i in range(g)
            ],
            axis=0,
        )
        acc_ref[...] += jnp.dot(left, right, preferred_element_type=jnp.float32)

    for n in range(kids):
        value = (-acc_ref[:, n * cols : (n + 1) * cols]).astype(slots_ref.dtype)
        wide_ref[pl.ds(n, depth, stride=kids), :] = value.astype(jnp.float32)
        for b in range(depth // BLK):
            at = slice(b * BLK, (b + 1) * BLK)
            kept = jnp.where(keep_ref[n, b] != 0, value[at], 0).astype(slots_ref.dtype)
            for h in range(HALVES):
                slots_ref[n * HALVES + h, at] = kept
    ainv_ref[...] = wide_ref[...].astype(ainv_ref.dtype)


def kid_product(slots_ref, panel_ref, part_ref):
    groups, depth, cols = slots_ref.shape
    n_row, tall, _ = part_ref.shape
    half = cols // HALVES
    c = panel_ref.shape[0] // CHUNKS
    right = slots_ref[...].reshape(groups * depth, cols)

    @pl.loop(0, CHUNKS)
    def _(s):
        left = jnp.concatenate(
            [
                jnp.concatenate(
                    [panel_ref[s * c + i, u * half : (u + 1) * half] for u in range(groups)],
                    axis=1,
                )
                for i in range(c)
            ],
            axis=0,
        )
        made = jnp.dot(left, right, preferred_element_type=jnp.float32).astype(part_ref.dtype)
        for i in range(c // 2):
            part_ref[s * (c // 2) + i] = made[i * tall : (i + 1) * tall]


def finish(pieces_ref, diag_ref, kk_ref, wide_ref):
    n_row, tall, cols = pieces_ref.shape
    depth = tall * HALVES
    kids = wide_ref.shape[0] // depth
    per = n_row // kids
    half = cols // HALVES
    wide_ref[...] = diag_ref[...].astype(jnp.float32)
    for n in range(kids):
        for h in range(HALVES):
            total = pieces_ref[n * per + h].astype(jnp.float32)
            for x in range(h + HALVES, per, HALVES):
                total += pieces_ref[n * per + x].astype(jnp.float32)
            for core in range(tall // half):
                at = pl.ds((core * cols + h * half) * kids + n, half, stride=kids)
                wide_ref[at, :] = wide_ref[at, :] - total[core * half : (core + 1) * half]
    kk_ref[...] = wide_ref[...].astype(kk_ref.dtype)


def body(root_inverse, factor, inverse_diag, structure):
    rows, kids, cols = factor.shape
    dtype = factor.dtype
    n_row, n_col = lax.axis_size("row"), lax.axis_size("col")
    per, side = rows // BLK, n_row // kids
    half, groups = cols // HALVES, kids * HALVES
    flat = (rows * kids, cols)
    along = [
        [y * side + x * HALVES + h for y in range(kids) for h in range(HALVES)]
        for x in range(side // HALVES)
    ]
    turned, folded = pl.pallas_call(
        split_kids,
        out_shape=(
            jax.ShapeDtypeStruct((groups, half, rows), dtype),
            jax.ShapeDtypeStruct((rows // 2, 2 * cols), dtype),
        ),
        in_specs=[ANY, ANY],
        out_specs=(VMEM, VMEM),
        scratch_shapes=[
            pltpu.VMEM(flat, dtype),
            pltpu.VMEM((rows, cols), dtype),
            pltpu.VMEM(flat, jnp.float32),
            pltpu.SemaphoreType.DMA((2,)),
        ],
        compiler_params=pltpu.CompilerParams(vmem_limit_bytes=VMEM_FIRST << 20),
    )(factor.reshape(flat), root_inverse)
    kid = lax.all_to_all(turned, "row", 0, 0, axis_index_groups=along)
    own = jnp.concatenate([kid.reshape(groups * half, rows), folded], axis=0)
    panel = lax.all_gather(own, "col", axis=0)
    keep = lax.dynamic_slice_in_dim(structure, lax.axis_index("row") * per, per, 1)
    mask = jnp.repeat(keep, BLK, axis=1).astype(dtype)
    masked = factor.transpose(1, 0, 2) * mask[:, :, None]
    row_m = lax.all_to_all(jnp.broadcast_to(masked[None], (n_row, kids, rows, cols)), "row", 0, 0)
    ainv, slots = pl.pallas_call(
        root_product,
        out_shape=(
            jax.ShapeDtypeStruct(flat, dtype),
            jax.ShapeDtypeStruct((groups, rows, cols), dtype),
        ),
        in_specs=[SMEM, ANY, ANY],
        out_specs=(VMEM, VMEM),
        scratch_shapes=[
            pltpu.VMEM((n_row, kids, rows, cols), dtype),
            pltpu.VMEM((n_col, rows // 2, 2 * cols), dtype),
            pltpu.VMEM((rows, kids * cols), jnp.float32),
            pltpu.VMEM(flat, jnp.float32),
            pltpu.SemaphoreType.DMA((2, CHUNKS)),
        ],
        compiler_params=pltpu.CompilerParams(vmem_limit_bytes=VMEM_ROOT << 20),
        cost_estimate=pl.CostEstimate(
            flops=2 * n_row * rows * rows * kids * cols,
            bytes_accessed=6 << 20,
            transcendentals=0,
        ),
    )(keep, row_m, panel)
    slots = lax.all_to_all(slots, "row", 0, 0, axis_index_groups=along)
    part = pl.pallas_call(
        kid_product,
        out_shape=jax.ShapeDtypeStruct((n_row, 2 * half, cols), dtype),
        in_specs=[VMEM, VMEM],
        out_specs=VMEM,
        compiler_params=pltpu.CompilerParams(vmem_limit_bytes=VMEM_KID << 20),
        cost_estimate=pl.CostEstimate(
            flops=2 * n_row * rows * rows * kids * cols,
            bytes_accessed=9 << 20,
            transcendentals=0,
        ),
    )(slots, panel)
    pieces = lax.all_to_all(part, "row", 0, 0)
    ainv_kk = pl.pallas_call(
        finish,
        out_shape=jax.ShapeDtypeStruct(flat, dtype),
        in_specs=[VMEM, VMEM],
        out_specs=VMEM,
        scratch_shapes=[pltpu.VMEM(flat, jnp.float32)],
        compiler_params=pltpu.CompilerParams(vmem_limit_bytes=6 << 20),
    )(pieces, inverse_diag.reshape(flat))
    return (ainv.reshape(factor.shape), ainv_kk.reshape(factor.shape))


def solution(mesh):
    return jax.shard_map(
        body,
        mesh=mesh,
        in_specs=(P("row", "col"), P("row", None, "col"), P("row", None, "col"), P()),
        out_specs=(P("row", None, "col"), P("row", None, "col")),
        check_vma=False,
    )
```

```python
import jax
import jax.numpy as jnp
from jax import lax
from jax.experimental import pallas as pl
from jax.experimental.pallas import tpu as pltpu
from jax.sharding import PartitionSpec as P

BLK = 128
CHUNKS = 4
KID_CHUNKS = 2
HALVES = 2
VMEM_FIRST, VMEM_ROOT, VMEM_KID = 63, 50, 16
ANY = pl.BlockSpec(memory_space=pl.ANY)
VMEM = pl.BlockSpec(memory_space=pltpu.VMEM)
SMEM = pl.BlockSpec(memory_space=pltpu.SMEM)


def split_kids(flat_ref, root_ref, turned_ref, folded_ref, flat_buf, root_buf, wide_ref, sems):
    groups, half, rows = turned_ref.shape
    kids = groups // HALVES
    cols = root_buf.shape[1]
    flat_copy = pltpu.make_async_copy(flat_ref, flat_buf, sems.at[0])
    root_copy = pltpu.make_async_copy(root_ref, root_buf, sems.at[1])
    flat_copy.start()
    root_copy.start()
    flat_copy.wait()
    wide_ref[...] = flat_buf[...].astype(jnp.float32)
    for n in range(kids):
        across = wide_ref[pl.ds(n, rows, stride=kids), :].astype(turned_ref.dtype).T
        for h in range(HALVES):
            turned_ref[n * HALVES + h] = across[h * half : (h + 1) * half]
    root_copy.wait()
    folded_ref[:, :cols] = root_buf[: rows // 2]
    folded_ref[:, cols:] = root_buf[rows // 2 :]


def root_product(
    keep_ref, row_ref, panel_ref, ainv_ref, slots_ref, row_buf, root_buf, acc_ref, wide_ref, sems
):
    n_row, kids, depth, cols = row_buf.shape
    first = panel_ref.shape[1] - root_buf.shape[1]
    g, c = n_row // CHUNKS, root_buf.shape[0] // CHUNKS

    def row_copy(s):
        return pltpu.make_async_copy(
            row_ref.at[pl.ds(s * g, g)], row_buf.at[pl.ds(s * g, g)], sems.at[0, s]
        )

    def root_copy(s):
        return pltpu.make_async_copy(
            panel_ref.at[pl.ds(s * c, c), pl.ds(first, root_buf.shape[1])],
            root_buf.at[pl.ds(s * c, c)],
            sems.at[1, s],
        )

    for s in range(CHUNKS):
        row_copy(s).start()
        root_copy(s).start()
    acc_ref[...] = jnp.zeros_like(acc_ref)

    @pl.loop(0, CHUNKS)
    def _(s):
        row_copy(s).wait()
        root_copy(s).wait()
        left = jnp.concatenate(
            [
                jnp.concatenate(
                    [root_buf[s * c + i, :, h * cols : (h + 1) * cols] for i in range(c)], axis=1
                )
                for h in range(2)
            ],
            axis=0,
        )
        right = jnp.concatenate(
            [
                jnp.concatenate([row_buf[s * g + i, n] for n in range(kids)], axis=1)
                for i in range(g)
            ],
            axis=0,
        )
        acc_ref[...] += jnp.dot(left, right, preferred_element_type=jnp.float32)

    for n in range(kids):
        value = (-acc_ref[:, n * cols : (n + 1) * cols]).astype(slots_ref.dtype)
        wide_ref[pl.ds(n, depth, stride=kids), :] = value.astype(jnp.float32)
        for b in range(depth // BLK):
            at = slice(b * BLK, (b + 1) * BLK)
            kept = jnp.where(keep_ref[n, b] != 0, value[at], 0).astype(slots_ref.dtype)
            for h in range(HALVES):
                slots_ref[n * HALVES + h, at] = kept
    ainv_ref[...] = wide_ref[...].astype(ainv_ref.dtype)


def kid_product(slots_ref, panel_ref, part_ref):
    groups, depth, cols = slots_ref.shape
    n_row, tall, _ = part_ref.shape
    half = cols // HALVES
    c = panel_ref.shape[0] // KID_CHUNKS
    right = slots_ref[...].reshape(groups * depth, cols)

    @pl.loop(0, KID_CHUNKS)
    def _(s):
        left = jnp.concatenate(
            [
                jnp.concatenate(
                    [panel_ref[s * c + i, u * half : (u + 1) * half] for u in range(groups)],
                    axis=1,
                )
                for i in range(c)
            ],
            axis=0,
        )
        made = jnp.dot(left, right, preferred_element_type=jnp.float32).astype(part_ref.dtype)
        for i in range(c // 2):
            part_ref[s * (c // 2) + i] = made[i * tall : (i + 1) * tall]


def finish(pieces_ref, diag_ref, kk_ref, wide_ref):
    n_row, tall, cols = pieces_ref.shape
    depth = tall * HALVES
    kids = wide_ref.shape[0] // depth
    per = n_row // kids
    half = cols // HALVES
    wide_ref[...] = diag_ref[...].astype(jnp.float32)
    for n in range(kids):
        for h in range(HALVES):
            total = pieces_ref[n * per + h].astype(jnp.float32)
            for x in range(h + HALVES, per, HALVES):
                total += pieces_ref[n * per + x].astype(jnp.float32)
            for core in range(tall // half):
                at = pl.ds((core * cols + h * half) * kids + n, half, stride=kids)
                wide_ref[at, :] = wide_ref[at, :] - total[core * half : (core + 1) * half]
    kk_ref[...] = wide_ref[...].astype(kk_ref.dtype)


def body(root_inverse, factor, inverse_diag, structure):
    rows, kids, cols = factor.shape
    dtype = factor.dtype
    n_row, n_col = lax.axis_size("row"), lax.axis_size("col")
    per, side = rows // BLK, n_row // kids
    half, groups = cols // HALVES, kids * HALVES
    flat = (rows * kids, cols)
    along = [
        [y * side + x * HALVES + h for y in range(kids) for h in range(HALVES)]
        for x in range(side // HALVES)
    ]
    turned, folded = pl.pallas_call(
        split_kids,
        out_shape=(
            jax.ShapeDtypeStruct((groups, half, rows), dtype),
            jax.ShapeDtypeStruct((rows // 2, 2 * cols), dtype),
        ),
        in_specs=[ANY, ANY],
        out_specs=(VMEM, VMEM),
        scratch_shapes=[
            pltpu.VMEM(flat, dtype),
            pltpu.VMEM((rows, cols), dtype),
            pltpu.VMEM(flat, jnp.float32),
            pltpu.SemaphoreType.DMA((2,)),
        ],
        compiler_params=pltpu.CompilerParams(vmem_limit_bytes=VMEM_FIRST << 20),
    )(factor.reshape(flat), root_inverse)
    kid = lax.all_to_all(turned, "row", 0, 0, axis_index_groups=along)
    own = jnp.concatenate([kid.reshape(groups * half, rows), folded], axis=0)
    panel = lax.all_gather(own, "col", axis=0)
    keep = lax.dynamic_slice_in_dim(structure, lax.axis_index("row") * per, per, 1)
    mask = jnp.repeat(keep, BLK, axis=1).astype(dtype)
    masked = factor.transpose(1, 0, 2) * mask[:, :, None]
    row_m = lax.all_to_all(jnp.broadcast_to(masked[None], (n_row, kids, rows, cols)), "row", 0, 0)
    ainv, slots = pl.pallas_call(
        root_product,
        out_shape=(
            jax.ShapeDtypeStruct(flat, dtype),
            jax.ShapeDtypeStruct((groups, rows, cols), dtype),
        ),
        in_specs=[SMEM, ANY, ANY],
        out_specs=(VMEM, VMEM),
        scratch_shapes=[
            pltpu.VMEM((n_row, kids, rows, cols), dtype),
            pltpu.VMEM((n_col, rows // 2, 2 * cols), dtype),
            pltpu.VMEM((rows, kids * cols), jnp.float32),
            pltpu.VMEM(flat, jnp.float32),
            pltpu.SemaphoreType.DMA((2, CHUNKS)),
        ],
        compiler_params=pltpu.CompilerParams(vmem_limit_bytes=VMEM_ROOT << 20),
        cost_estimate=pl.CostEstimate(
            flops=2 * n_row * rows * rows * kids * cols,
            bytes_accessed=6 << 20,
            transcendentals=0,
        ),
    )(keep, row_m, panel)
    slots = lax.all_to_all(slots, "row", 0, 0, axis_index_groups=along)
    part = pl.pallas_call(
        kid_product,
        out_shape=jax.ShapeDtypeStruct((n_row, 2 * half, cols), dtype),
        in_specs=[VMEM, VMEM],
        out_specs=VMEM,
        compiler_params=pltpu.CompilerParams(vmem_limit_bytes=VMEM_KID << 20),
        cost_estimate=pl.CostEstimate(
            flops=2 * n_row * rows * rows * kids * cols,
            bytes_accessed=9 << 20,
            transcendentals=0,
        ),
    )(slots, panel)
    pieces = lax.all_to_all(part, "row", 0, 0)
    ainv_kk = pl.pallas_call(
        finish,
        out_shape=jax.ShapeDtypeStruct(flat, dtype),
        in_specs=[VMEM, VMEM],
        out_specs=VMEM,
        scratch_shapes=[pltpu.VMEM(flat, jnp.float32)],
        compiler_params=pltpu.CompilerParams(vmem_limit_bytes=6 << 20),
    )(pieces, inverse_diag.reshape(flat))
    return (ainv.reshape(factor.shape), ainv_kk.reshape(factor.shape))


def solution(mesh):
    return jax.shard_map(
        body,
        mesh=mesh,
        in_specs=(P("row", "col"), P("row", None, "col"), P("row", None, "col"), P()),
        out_specs=(P("row", None, "col"), P("row", None, "col")),
        check_vma=False,
    )
```

```python
import jax
import jax.numpy as jnp
from jax import lax
from jax.experimental import pallas as pl
from jax.experimental.pallas import tpu as pltpu
from jax.sharding import PartitionSpec as P

BLK = 128
CHUNKS = 4
KID_CHUNKS = 2
HALVES = 2
VMEM_FIRST, VMEM_ROOT, VMEM_KID = 63, 50, 16
ANY = pl.BlockSpec(memory_space=pl.ANY)
VMEM = pl.BlockSpec(memory_space=pltpu.VMEM)
SMEM = pl.BlockSpec(memory_space=pltpu.SMEM)


def split_kids(
    flat_ref, root_ref, turned_ref, own_ref, flat_buf, root_buf, folded_ref, wide_ref, turned_buf, sems
):
    groups, half, rows = turned_buf.shape
    kids = groups // HALVES
    cols = root_buf.shape[1]
    flat_copy = pltpu.make_async_copy(flat_ref, flat_buf, sems.at[0])
    root_copy = pltpu.make_async_copy(root_ref, root_buf, sems.at[1])
    flat_copy.start()
    root_copy.start()
    root_copy.wait()
    folded_ref[:, :cols] = root_buf[: rows // 2]
    folded_ref[:, cols:] = root_buf[rows // 2 :]
    at = pl.ds(own_ref.shape[0] - rows // 2, rows // 2)
    own_copy = pltpu.make_async_copy(folded_ref, own_ref.at[at], sems.at[2])
    own_copy.start()
    flat_copy.wait()
    wide_ref[...] = flat_buf[...].astype(jnp.float32)
    for n in range(kids):
        across = wide_ref[pl.ds(n, rows, stride=kids), :].astype(turned_ref.dtype).T
        for h in range(HALVES):
            turned_buf[n * HALVES + h] = across[h * half : (h + 1) * half]
    turned_copy = pltpu.make_async_copy(turned_buf, turned_ref, sems.at[3])
    turned_copy.start()
    own_copy.wait()
    turned_copy.wait()


def root_product(
    keep_ref, row_ref, panel_ref, ainv_ref, slots_ref, row_buf, root_buf, acc_ref, wide_ref, sems
):
    n_row, kids, depth, cols = row_buf.shape
    first = panel_ref.shape[1] - root_buf.shape[1]
    g, c = n_row // CHUNKS, root_buf.shape[0] // CHUNKS

    def row_copy(s):
        return pltpu.make_async_copy(
            row_ref.at[pl.ds(s * g, g)], row_buf.at[pl.ds(s * g, g)], sems.at[0, s]
        )

    def root_copy(s):
        return pltpu.make_async_copy(
            panel_ref.at[pl.ds(s * c, c), pl.ds(first, root_buf.shape[1])],
            root_buf.at[pl.ds(s * c, c)],
            sems.at[1, s],
        )

    for s in range(CHUNKS):
        row_copy(s).start()
        root_copy(s).start()
    acc_ref[...] = jnp.zeros_like(acc_ref)

    @pl.loop(0, CHUNKS)
    def _(s):
        row_copy(s).wait()
        root_copy(s).wait()
        left = jnp.concatenate(
            [
                jnp.concatenate(
                    [root_buf[s * c + i, :, h * cols : (h + 1) * cols] for i in range(c)], axis=1
                )
                for h in range(2)
            ],
            axis=0,
        )
        right = jnp.concatenate(
            [
                jnp.concatenate([row_buf[s * g + i, n] for n in range(kids)], axis=1)
                for i in range(g)
            ],
            axis=0,
        )
        acc_ref[...] += jnp.dot(left, right, preferred_element_type=jnp.float32)

    for n in range(kids):
        value = (-acc_ref[:, n * cols : (n + 1) * cols]).astype(slots_ref.dtype)
        wide_ref[pl.ds(n, depth, stride=kids), :] = value.astype(jnp.float32)
        for b in range(depth // BLK):
            at = slice(b * BLK, (b + 1) * BLK)
            kept = jnp.where(keep_ref[n, b] != 0, value[at], 0).astype(slots_ref.dtype)
            for h in range(HALVES):
                slots_ref[n * HALVES + h, at] = kept
    ainv_ref[...] = wide_ref[...].astype(ainv_ref.dtype)


def kid_product(slots_ref, panel_ref, part_ref):
    groups, depth, cols = slots_ref.shape
    n_row, tall, _ = part_ref.shape
    half = cols // HALVES
    c = panel_ref.shape[0] // KID_CHUNKS
    right = slots_ref[...].reshape(groups * depth, cols)

    @pl.loop(0, KID_CHUNKS)
    def _(s):
        left = jnp.concatenate(
            [
                jnp.concatenate(
                    [panel_ref[s * c + i, u * half : (u + 1) * half] for u in range(groups)],
                    axis=1,
                )
                for i in range(c)
            ],
            axis=0,
        )
        made = jnp.dot(left, right, preferred_element_type=jnp.float32).astype(part_ref.dtype)
        for i in range(c // 2):
            part_ref[s * (c // 2) + i] = made[i * tall : (i + 1) * tall]


def finish(pieces_ref, diag_ref, kk_ref, wide_ref):
    n_row, tall, cols = pieces_ref.shape
    depth = tall * HALVES
    kids = wide_ref.shape[0] // depth
    per = n_row // kids
    half = cols // HALVES
    wide_ref[...] = diag_ref[...].astype(jnp.float32)
    for n in range(kids):
        for h in range(HALVES):
            total = pieces_ref[n * per + h].astype(jnp.float32)
            for x in range(h + HALVES, per, HALVES):
                total += pieces_ref[n * per + x].astype(jnp.float32)
            for core in range(tall // half):
                at = pl.ds((core * cols + h * half) * kids + n, half, stride=kids)
                wide_ref[at, :] = wide_ref[at, :] - total[core * half : (core + 1) * half]
    kk_ref[...] = wide_ref[...].astype(kk_ref.dtype)


def body(root_inverse, factor, inverse_diag, structure):
    rows, kids, cols = factor.shape
    dtype = factor.dtype
    n_row, n_col = lax.axis_size("row"), lax.axis_size("col")
    per, side = rows // BLK, n_row // kids
    half, groups = cols // HALVES, kids * HALVES
    flat = (rows * kids, cols)
    along = [
        [y * side + x * HALVES + h for y in range(kids) for h in range(HALVES)]
        for x in range(side // HALVES)
    ]
    turned, own = pl.pallas_call(
        split_kids,
        out_shape=(
            jax.ShapeDtypeStruct((groups, half, rows), dtype),
            jax.ShapeDtypeStruct((groups * half + rows // 2, rows), dtype),
        ),
        in_specs=[ANY, ANY],
        out_specs=(ANY, ANY),
        scratch_shapes=[
            pltpu.VMEM(flat, dtype),
            pltpu.VMEM((rows, cols), dtype),
            pltpu.VMEM((rows // 2, 2 * cols), dtype),
            pltpu.VMEM(flat, jnp.float32),
            pltpu.VMEM((groups, half, rows), dtype),
            pltpu.SemaphoreType.DMA((4,)),
        ],
        compiler_params=pltpu.CompilerParams(vmem_limit_bytes=VMEM_FIRST << 20),
    )(factor.reshape(flat), root_inverse)
    kid = lax.all_to_all(turned, "row", 0, 0, axis_index_groups=along)
    own = lax.dynamic_update_slice(own, kid.reshape(groups * half, rows), (0, 0))
    panel = lax.all_gather(own, "col", axis=0)
    keep = lax.dynamic_slice_in_dim(structure, lax.axis_index("row") * per, per, 1)
    mask = jnp.repeat(keep, BLK, axis=1).astype(dtype)
    masked = factor.transpose(1, 0, 2) * mask[:, :, None]
    row_m = lax.all_to_all(jnp.broadcast_to(masked[None], (n_row, kids, rows, cols)), "row", 0, 0)
    ainv, slots = pl.pallas_call(
        root_product,
        out_shape=(
            jax.ShapeDtypeStruct(flat, dtype),
            jax.ShapeDtypeStruct((groups, rows, cols), dtype),
        ),
        in_specs=[SMEM, ANY, ANY],
        out_specs=(VMEM, VMEM),
        scratch_shapes=[
            pltpu.VMEM((n_row, kids, rows, cols), dtype),
            pltpu.VMEM((n_col, rows // 2, 2 * cols), dtype),
            pltpu.VMEM((rows, kids * cols), jnp.float32),
            pltpu.VMEM(flat, jnp.float32),
            pltpu.SemaphoreType.DMA((2, CHUNKS)),
        ],
        compiler_params=pltpu.CompilerParams(vmem_limit_bytes=VMEM_ROOT << 20),
        cost_estimate=pl.CostEstimate(
            flops=2 * n_row * rows * rows * kids * cols,
            bytes_accessed=6 << 20,
            transcendentals=0,
        ),
    )(keep, row_m, panel)
    slots = lax.all_to_all(slots, "row", 0, 0, axis_index_groups=along)
    part = pl.pallas_call(
        kid_product,
        out_shape=jax.ShapeDtypeStruct((n_row, 2 * half, cols), dtype),
        in_specs=[VMEM, VMEM],
        out_specs=VMEM,
        compiler_params=pltpu.CompilerParams(vmem_limit_bytes=VMEM_KID << 20),
        cost_estimate=pl.CostEstimate(
            flops=2 * n_row * rows * rows * kids * cols,
            bytes_accessed=9 << 20,
            transcendentals=0,
        ),
    )(slots, panel)
    pieces = lax.all_to_all(part, "row", 0, 0)
    ainv_kk = pl.pallas_call(
        finish,
        out_shape=jax.ShapeDtypeStruct(flat, dtype),
        in_specs=[VMEM, VMEM],
        out_specs=VMEM,
        scratch_shapes=[pltpu.VMEM(flat, jnp.float32)],
        compiler_params=pltpu.CompilerParams(vmem_limit_bytes=6 << 20),
    )(pieces, inverse_diag.reshape(flat))
    return (ainv.reshape(factor.shape), ainv_kk.reshape(factor.shape))


def solution(mesh):
    return jax.shard_map(
        body,
        mesh=mesh,
        in_specs=(P("row", "col"), P("row", None, "col"), P("row", None, "col"), P()),
        out_specs=(P("row", None, "col"), P("row", None, "col")),
        check_vma=False,
    )
```

```python
import jax
import jax.numpy as jnp
from jax import lax
from jax.experimental import pallas as pl
from jax.experimental.pallas import tpu as pltpu
from jax.sharding import PartitionSpec as P

BLK = 128
CHUNKS = 4
KID_CHUNKS = 2
HALVES = 2
VMEM_FIRST, VMEM_ROOT, VMEM_KID = 63, 50, 16
ANY = pl.BlockSpec(memory_space=pl.ANY)
VMEM = pl.BlockSpec(memory_space=pltpu.VMEM)
SMEM = pl.BlockSpec(memory_space=pltpu.SMEM)


def split_kids(
    flat_ref, root_ref, turned_ref, own_ref, flat_buf, root_buf, folded_ref, wide_ref, turned_buf, sems
):
    groups, half, rows = turned_buf.shape
    kids = groups // HALVES
    cols = root_buf.shape[1]
    flat_copy = pltpu.make_async_copy(flat_ref, flat_buf, sems.at[0])
    root_copy = pltpu.make_async_copy(root_ref, root_buf, sems.at[1])
    flat_copy.start()
    root_copy.start()
    root_copy.wait()
    folded_ref[:, :cols] = root_buf[: rows // 2]
    folded_ref[:, cols:] = root_buf[rows // 2 :]
    at = pl.ds(own_ref.shape[0] - rows // 2, rows // 2)
    own_copy = pltpu.make_async_copy(folded_ref, own_ref.at[at], sems.at[2])
    own_copy.start()
    flat_copy.wait()
    wide_ref[...] = flat_buf[...].astype(jnp.float32)
    for n in range(kids):
        across = wide_ref[pl.ds(n, rows, stride=kids), :].astype(turned_ref.dtype).T
        for h in range(HALVES):
            turned_buf[n * HALVES + h] = across[h * half : (h + 1) * half]
    turned_copy = pltpu.make_async_copy(turned_buf, turned_ref, sems.at[3])
    turned_copy.start()
    own_copy.wait()
    turned_copy.wait()


def root_product(
    keep_ref, row_ref, panel_ref, ainv_ref, slots_ref, row_buf, root_buf, acc_ref, wide_ref, ainv_buf, sems, out_sem
):
    n_row, kids, depth, cols = row_buf.shape
    first = panel_ref.shape[1] - root_buf.shape[1]
    g, c = n_row // CHUNKS, root_buf.shape[0] // CHUNKS

    def row_copy(s):
        return pltpu.make_async_copy(
            row_ref.at[pl.ds(s * g, g)], row_buf.at[pl.ds(s * g, g)], sems.at[0, s]
        )

    def root_copy(s):
        return pltpu.make_async_copy(
            panel_ref.at[pl.ds(s * c, c), pl.ds(first, root_buf.shape[1])],
            root_buf.at[pl.ds(s * c, c)],
            sems.at[1, s],
        )

    for s in range(CHUNKS):
        row_copy(s).start()
        root_copy(s).start()
    acc_ref[...] = jnp.zeros_like(acc_ref)

    @pl.loop(0, CHUNKS)
    def _(s):
        row_copy(s).wait()
        root_copy(s).wait()
        left = jnp.concatenate(
            [
                jnp.concatenate(
                    [root_buf[s * c + i, :, h * cols : (h + 1) * cols] for i in range(c)], axis=1
                )
                for h in range(2)
            ],
            axis=0,
        )
        right = jnp.concatenate(
            [
                jnp.concatenate([row_buf[s * g + i, n] for n in range(kids)], axis=1)
                for i in range(g)
            ],
            axis=0,
        )
        acc_ref[...] += jnp.dot(left, right, preferred_element_type=jnp.float32)

    for n in range(kids):
        value = (-acc_ref[:, n * cols : (n + 1) * cols]).astype(slots_ref.dtype)
        wide_ref[pl.ds(n, depth, stride=kids), :] = value.astype(jnp.float32)
    ainv_buf[...] = wide_ref[...].astype(ainv_buf.dtype)
    ainv_copy = pltpu.make_async_copy(ainv_buf, ainv_ref, out_sem)
    ainv_copy.start()
    for n in range(kids):
        value = (-acc_ref[:, n * cols : (n + 1) * cols]).astype(slots_ref.dtype)
        for b in range(depth // BLK):
            at = slice(b * BLK, (b + 1) * BLK)
            kept = jnp.where(keep_ref[n, b] != 0, value[at], 0).astype(slots_ref.dtype)
            for h in range(HALVES):
                slots_ref[n * HALVES + h, at] = kept
    ainv_copy.wait()


def kid_product(slots_ref, panel_ref, part_ref):
    groups, depth, cols = slots_ref.shape
    n_row, tall, _ = part_ref.shape
    half = cols // HALVES
    c = panel_ref.shape[0] // KID_CHUNKS
    right = slots_ref[...].reshape(groups * depth, cols)

    @pl.loop(0, KID_CHUNKS)
    def _(s):
        left = jnp.concatenate(
            [
                jnp.concatenate(
                    [panel_ref[s * c + i, u * half : (u + 1) * half] for u in range(groups)],
                    axis=1,
                )
                for i in range(c)
            ],
            axis=0,
        )
        made = jnp.dot(left, right, preferred_element_type=jnp.float32).astype(part_ref.dtype)
        for i in range(c // 2):
            part_ref[s * (c // 2) + i] = made[i * tall : (i + 1) * tall]


def finish(pieces_ref, diag_ref, kk_ref, wide_ref):
    n_row, tall, cols = pieces_ref.shape
    depth = tall * HALVES
    kids = wide_ref.shape[0] // depth
    per = n_row // kids
    half = cols // HALVES
    wide_ref[...] = diag_ref[...].astype(jnp.float32)
    for n in range(kids):
        for h in range(HALVES):
            total = pieces_ref[n * per + h].astype(jnp.float32)
            for x in range(h + HALVES, per, HALVES):
                total += pieces_ref[n * per + x].astype(jnp.float32)
            for core in range(tall // half):
                at = pl.ds((core * cols + h * half) * kids + n, half, stride=kids)
                wide_ref[at, :] = wide_ref[at, :] - total[core * half : (core + 1) * half]
    kk_ref[...] = wide_ref[...].astype(kk_ref.dtype)


def body(root_inverse, factor, inverse_diag, structure):
    rows, kids, cols = factor.shape
    dtype = factor.dtype
    n_row, n_col = lax.axis_size("row"), lax.axis_size("col")
    per, side = rows // BLK, n_row // kids
    half, groups = cols // HALVES, kids * HALVES
    flat = (rows * kids, cols)
    along = [
        [y * side + x * HALVES + h for y in range(kids) for h in range(HALVES)]
        for x in range(side // HALVES)
    ]
    turned, own = pl.pallas_call(
        split_kids,
        out_shape=(
            jax.ShapeDtypeStruct((groups, half, rows), dtype),
            jax.ShapeDtypeStruct((groups * half + rows // 2, rows), dtype),
        ),
        in_specs=[ANY, ANY],
        out_specs=(ANY, ANY),
        scratch_shapes=[
            pltpu.VMEM(flat, dtype),
            pltpu.VMEM((rows, cols), dtype),
            pltpu.VMEM((rows // 2, 2 * cols), dtype),
            pltpu.VMEM(flat, jnp.float32),
            pltpu.VMEM((groups, half, rows), dtype),
            pltpu.SemaphoreType.DMA((4,)),
        ],
        compiler_params=pltpu.CompilerParams(vmem_limit_bytes=VMEM_FIRST << 20),
    )(factor.reshape(flat), root_inverse)
    kid = lax.all_to_all(turned, "row", 0, 0, axis_index_groups=along)
    own = lax.dynamic_update_slice(own, kid.reshape(groups * half, rows), (0, 0))
    panel = lax.all_gather(own, "col", axis=0)
    keep = lax.dynamic_slice_in_dim(structure, lax.axis_index("row") * per, per, 1)
    mask = jnp.repeat(keep, BLK, axis=1).astype(dtype)
    masked = factor.transpose(1, 0, 2) * mask[:, :, None]
    row_m = lax.all_to_all(jnp.broadcast_to(masked[None], (n_row, kids, rows, cols)), "row", 0, 0)
    ainv, slots = pl.pallas_call(
        root_product,
        out_shape=(
            jax.ShapeDtypeStruct(flat, dtype),
            jax.ShapeDtypeStruct((groups, rows, cols), dtype),
        ),
        in_specs=[SMEM, ANY, ANY],
        out_specs=(ANY, VMEM),
        scratch_shapes=[
            pltpu.VMEM((n_row, kids, rows, cols), dtype),
            pltpu.VMEM((n_col, rows // 2, 2 * cols), dtype),
            pltpu.VMEM((rows, kids * cols), jnp.float32),
            pltpu.VMEM(flat, jnp.float32),
            pltpu.VMEM(flat, dtype),
            pltpu.SemaphoreType.DMA((2, CHUNKS)),
            pltpu.SemaphoreType.DMA(()),
        ],
        compiler_params=pltpu.CompilerParams(vmem_limit_bytes=VMEM_ROOT << 20),
        cost_estimate=pl.CostEstimate(
            flops=2 * n_row * rows * rows * kids * cols,
            bytes_accessed=6 << 20,
            transcendentals=0,
        ),
    )(keep, row_m, panel)
    slots = lax.all_to_all(slots, "row", 0, 0, axis_index_groups=along)
    part = pl.pallas_call(
        kid_product,
        out_shape=jax.ShapeDtypeStruct((n_row, 2 * half, cols), dtype),
        in_specs=[VMEM, VMEM],
        out_specs=VMEM,
        compiler_params=pltpu.CompilerParams(vmem_limit_bytes=VMEM_KID << 20),
        cost_estimate=pl.CostEstimate(
            flops=2 * n_row * rows * rows * kids * cols,
            bytes_accessed=9 << 20,
            transcendentals=0,
        ),
    )(slots, panel)
    pieces = lax.all_to_all(part, "row", 0, 0)
    ainv_kk = pl.pallas_call(
        finish,
        out_shape=jax.ShapeDtypeStruct(flat, dtype),
        in_specs=[VMEM, VMEM],
        out_specs=VMEM,
        scratch_shapes=[pltpu.VMEM(flat, jnp.float32)],
        compiler_params=pltpu.CompilerParams(vmem_limit_bytes=6 << 20),
    )(pieces, inverse_diag.reshape(flat))
    return (ainv.reshape(factor.shape), ainv_kk.reshape(factor.shape))


def solution(mesh):
    return jax.shard_map(
        body,
        mesh=mesh,
        in_specs=(P("row", "col"), P("row", None, "col"), P("row", None, "col"), P()),
        out_specs=(P("row", None, "col"), P("row", None, "col")),
        check_vma=False,
    )
```
